32 devices in a mesh: gx: 4 (over y, x), gy: 8 (over z, core).
Axes of the slice: x: 2, y: 2, z: 4, core: 2. Of those that a mesh axis runs over, the one named last changes fastest.
Arguments:
- posterior: bfloat16 [8192, 1000], P(('gx', 'gy')), may hold values from -6 to 6
- class_affinity: bfloat16 [8192, 1000], P(('gx', 'gy')), may hold values from 0.049804688 to 20
- band_tiles: bfloat16 [64, 4, 128, 128], P(('gx', 'gy')), may hold values from 9.9658966e-05 to 1
- band_offset: int32 [64, 4], P(('gx', 'gy')), may hold values from -1 to 1
- band_count: int32 [64], P(('gx', 'gy')), may hold values from 1 to 4
- far_tiles: bfloat16 [32, 4, 128, 128], P(('gx', 'gy')), may hold values from 9.9658966e-05 to 1
- far_row: int32 [32, 4], P(('gx', 'gy')), may hold values from 0 to 1
- far_block: int32 [32, 4], P(('gx', 'gy')), may hold values from 0 to 1
Outputs:
- propagated: bfloat16 [8192, 1000], P(('gx', 'gy'))
The draws below stay inside these ranges and needn't reach their ends.
Inputs may be any that keep to these rules, and one draw needn't show every extreme that they name: Near tiles of a slot index at or above band_count of their row block are not part of the graph.
All inputs are finite; a program needn't handle non-finite values.
Results may differ from the reference program's by a relative error of at most 0.002.
Values may be sent and summed in bfloat16 or wider, within the bound.
A program may use at most 64 MiB of HBM per device.

```python
import math
import jax
import jax.numpy as jnp
from jax import lax

CLASSES = 1000
TILE_SIZE = 128
BLOCKS_DEV = 2
SLOTS = 4
BAND_REACH = 1
SWEEPS = 2
ALL_BLOCKS = 64
ALL_NODES = 8192
N_GX = 4
N_GY = 8
DEVICES = 32


def touch_ends(result, own_key, low, top_value):
    longest = result.shape.index(max(result.shape))
    spots = []
    for shift in (0, 1):
        where = [jax.random.randint(jax.random.fold_in(own_key, axis), (), 0, length) for axis, length in enumerate(result.shape)]
        where[longest] = (where[longest] + shift) % result.shape[longest]
        spots.append(tuple(where))
    return result.at[spots[0]].set(low).at[spots[1]].set(top_value)


def block_levels(stream_key, shape, shards, low, largest):
    def one(axis_at, blocks):
        draws = jax.random.uniform(jax.random.fold_in(jax.random.fold_in(stream_key, 6), axis_at), (blocks,), jnp.float32, low / len(shards), largest / len(shards))
        return jnp.repeat(jnp.exp(draws), shape[axis_at] // blocks).reshape((-1,) + (1,) * (len(shape) - axis_at - 1))

    factor_of = one(*shards[0])
    for cut in shards[1:]:
        factor_of = factor_of * one(*cut)
    return factor_of


def scatter_about(own_key, dims, deviation, most, cuts=(), kind=jnp.bfloat16):
    drawn = jax.random.normal(own_key, dims, jnp.float32) * deviation
    if len(cuts) > 0:
        drawn = block_levels(own_key, dims, cuts, -0.22, 0.18) * drawn
    return jnp.clip(drawn, min=-most, max=most).astype(kind)


def setup_inputs(seed: int = 0) -> dict:
    splits = jax.random.split(jax.random.key(seed), 9)
    posterior = scatter_about(splits[0], (ALL_NODES, CLASSES), 1.0, 6.0, ((0, 32),))
    class_affinity = jnp.clip(jnp.exp(math.log(20.0) - 5.9953784 * jax.random.uniform(splits[1], (ALL_NODES, CLASSES), jnp.float32) ** block_levels(splits[1], (ALL_NODES, CLASSES), ((0, 32),), -0.2, 0.2)), 0.049804688, 20.0).astype(jnp.bfloat16)
    band_tiles = jnp.clip(jnp.exp(math.log(1.0) - 9.213757 * jax.random.uniform(splits[2], (ALL_BLOCKS, SLOTS, TILE_SIZE, TILE_SIZE), jnp.float32) ** block_levels(splits[2], (ALL_BLOCKS, SLOTS, TILE_SIZE, TILE_SIZE), ((0, 32),), -0.2, 0.2)), 9.965896606445312e-05, 1.0).astype(jnp.bfloat16)
    band_offset = touch_ends(jax.random.randint(splits[3], (ALL_BLOCKS, SLOTS), 0 - BAND_REACH, BAND_REACH + 1), jax.random.fold_in(splits[3], 1), 0 - BAND_REACH, BAND_REACH).astype(jnp.int32)
    band_count = touch_ends(jax.random.randint(splits[4], (ALL_BLOCKS,), 1, SLOTS + 1), jax.random.fold_in(splits[4], 1), 1, SLOTS).astype(jnp.int32)
    far_tiles = jnp.clip(jnp.exp(math.log(1.0) - 9.213757 * jax.random.uniform(splits[5], (DEVICES, N_GX, TILE_SIZE, TILE_SIZE), jnp.float32) ** block_levels(splits[5], (DEVICES, N_GX, TILE_SIZE, TILE_SIZE), ((0, 32),), -0.2, 0.2)), 9.965896606445312e-05, 1.0).astype(jnp.bfloat16)
    far_row = touch_ends(jax.random.randint(splits[6], (DEVICES, N_GX), 0, BLOCKS_DEV), jax.random.fold_in(splits[6], 1), 0, BLOCKS_DEV - 1).astype(jnp.int32)
    far_block = touch_ends(jax.random.randint(splits[7], (DEVICES, N_GX), 0, BLOCKS_DEV), jax.random.fold_in(splits[7], 1), 0, BLOCKS_DEV - 1).astype(jnp.int32)
    return dict(posterior=posterior, class_affinity=class_affinity, band_tiles=band_tiles, band_offset=band_offset, band_count=band_count, far_tiles=far_tiles, far_row=far_row, far_block=far_block)


propagation_weight = 0.9
epsilon = 1e-06

def normalize(mixed_rows):
    row_scale = lax.rsqrt(lax.optimization_barrier(jnp.mean(mixed_rows * mixed_rows, axis=-1, keepdims=True)) + epsilon)
    return (mixed_rows * row_scale).astype(jnp.bfloat16)

def reference(posterior, class_affinity, band_tiles, band_offset, band_count, far_tiles, far_row, far_block):
    class_count = posterior.shape[1]
    device_count = N_GX * N_GY
    group_blocks = BLOCKS_DEV * N_GY
    slot_ids = jnp.arange(SLOTS, dtype=jnp.int32)
    peer_ids = jnp.arange(N_GX, dtype=jnp.int32)
    block_ids = jnp.arange(BLOCKS_DEV, dtype=jnp.int32)
    current = posterior
    for sweep in range(SWEEPS):
        blocks_all = current.reshape(device_count * BLOCKS_DEV, TILE_SIZE, class_count)

        def one_device(device):
            device = device.astype(jnp.int32)
            outer_index = device // N_GY
            inner_index = device % N_GY
            first_block = device * BLOCKS_DEV
            rows_here = first_block + block_ids
            tile_block = lax.dynamic_slice_in_dim(band_tiles, first_block, BLOCKS_DEV, 0)
            offsets = lax.dynamic_slice_in_dim(band_offset, first_block, BLOCKS_DEV, 0)
            counts = lax.dynamic_slice_in_dim(band_count, first_block, BLOCKS_DEV, 0)
            group_base = outer_index * group_blocks
            columns = (group_base + (rows_here[:, None] - group_base + offsets) % group_blocks).astype(jnp.int32)
            live_mask = (slot_ids[None, :] < counts[:, None]).astype(jnp.float32)
            sources = blocks_all[columns]
            band_sum = jnp.einsum('bsij,bsjc->bic', tile_block.astype(jnp.float32) * live_mask[:, :, None, None], sources.astype(jnp.float32))
            far_block_tiles = far_tiles[device]
            far_rows = far_row[device]
            far_source = far_block[device]
            far_columns = ((peer_ids * N_GY + inner_index) * BLOCKS_DEV + far_source).astype(jnp.int32)
            far_sources = blocks_all[far_columns]
            far_parts = jnp.einsum('qij,qjc->qic', far_block_tiles.astype(jnp.float32), far_sources.astype(jnp.float32))
            owner_table = (far_rows[None, :] == block_ids[:, None]).astype(jnp.float32)
            far_sum = jnp.einsum('bq,qic->bic', owner_table, far_parts)
            combined = (band_sum + far_sum).reshape(BLOCKS_DEV * TILE_SIZE, class_count)
            affinity_rows = lax.dynamic_slice_in_dim(class_affinity, first_block * TILE_SIZE, BLOCKS_DEV * TILE_SIZE, 0)
            mixed_rows = propagation_weight * combined + affinity_rows.astype(jnp.float32)
            return normalize(mixed_rows)
        current = lax.map(one_device, jnp.arange(device_count, dtype=jnp.int32)).reshape(device_count * BLOCKS_DEV * TILE_SIZE, class_count)
    return current
```

```python
import functools

import jax
import jax.numpy as jnp
from jax import lax
from jax.experimental import pallas as pl
from jax.experimental.pallas import tpu as pltpu
from jax.sharding import PartitionSpec as P

SWEEPS = 2
propagation_weight = 0.9
epsilon = 1e-06
SHARE = 0.32
HALVES = 1
DIRECT = 2
MESH = pl.DeviceIdType.MESH


def partner(me, step, peers):
    total = 0
    bit = 1
    while bit < peers:
        here = lax.rem(me // bit, 2)
        total = total + bit * (lax.rem(here + 1, 2) if step & bit else here)
        bit *= 2
    return total


def split(first, size, pieces):
    step = -(-size // (pieces * 16)) * 16
    return [(c, min(step, first + size - c)) for c in range(first, first + size, step)]


def chunks_of(classes, peers):
    cuts = []
    first = 0
    if peers == 4:
        share = int(classes * SHARE) // 16 * 16
        if share:
            for via in (1, 2):
                cuts += [(c, w, via) for c, w in split(first, share, HALVES)]
                first += share
    cuts += [(c, w, 0) for c, w in split(first, classes - first, DIRECT)]
    return cuts


def order_of(cuts):
    direct = [k for k, cut in enumerate(cuts) if cut[2] == 0]
    one = [k for k, cut in enumerate(cuts) if cut[2] == 1]
    two = [k for k, cut in enumerate(cuts) if cut[2] == 2]
    return direct[:-1] + [k for pair in zip(one, two) for k in pair] + direct[-1:]


def kernel(
    peers, ring, cuts,
    post, aff_hbm, band_hbm, far_hbm, boff_hbm, bcnt_hbm, frow_hbm, fblk_hbm,
    out,
    own, exts, pairs, stage, arrived, gauge, scale_gauge, asked, aff, band, far, near_weights, far_weights, acc,
    boff, bcnt, frow, fblk, scales, own_scale, far_scale_out, far_scale_in,
    load_sem, ask_sem, pair_sem, halo_send, far_send, halo_recv, far_recv, scale_sem,
):
    me = lax.axis_index("gx")
    spot = lax.axis_index("gy")
    up = lax.rem(spot + 1, ring)
    down = lax.rem(spot + ring - 1, ring)
    blocks, slots, tile, _ = band.shape
    classes = post.shape[0]
    steps = list(range(1, peers))
    mates = {r: partner(me, r, peers) for r in range(peers)}
    order = order_of(cuts)
    early = [k for k, cut in enumerate(cuts) if cut[2]]

    barrier = pltpu.get_barrier_semaphore()
    for r in steps:
        pl.semaphore_signal(barrier, inc=1, device_id={"gx": mates[r]}, device_id_type=MESH)
    for side in (up, down):
        pl.semaphore_signal(barrier, inc=1, device_id={"gy": side}, device_id_type=MESH)

    pending = []

    def load(source, target):
        copy = pltpu.make_async_copy(source, target, load_sem.at[len(pending)])
        copy.start()
        pending.append(copy)
        return copy

    mine = [load(post.at[:, pl.ds(b * tile, tile)], own[0].at[b]) for b in range(blocks)]
    words = [
        load(source, target)
        for source, target in ((fblk_hbm, fblk), (frow_hbm, frow), (bcnt_hbm, bcnt), (boff_hbm, boff))
    ]
    band_load = load(band_hbm, band)
    far_load = load(far_hbm, far)
    aff_load = load(aff_hbm, aff)

    def drain(whole, sem):
        pltpu.make_async_copy(whole, whole, sem).wait()

    def several(copies, first, size):
        return gauge.at[pl.ds(0, copies), pl.ds(first, size)]

    def to_mate(r, source, target, send, recv):
        return pltpu.make_async_remote_copy(
            src_ref=source, dst_ref=target, send_sem=send, recv_sem=recv,
            device_id={"gx": mates[r]}, device_id_type=MESH,
        )

    def to_sides(first, last, before, after, send, recv):
        for source, target, side in ((last, before, up), (first, after, down)):
            pltpu.make_async_remote_copy(
                src_ref=source, dst_ref=target, send_sem=send, recv_sem=recv,
                device_id={"gy": side}, device_id_type=MESH,
            ).start()

    def send_halo(sweep, k):
        c, w, _ = cuts[k]
        to_sides(
            own[sweep].at[0, pl.ds(c, w)], own[sweep].at[blocks - 1, pl.ds(c, w)],
            exts[sweep][k].at[0], exts[sweep][k].at[blocks + 1],
            halo_send.at[sweep], halo_recv.at[sweep, k],
        )

    def send_far(sweep, k, mates_of):
        c, w, _ = cuts[k]
        rows = pl.ds(c, w)
        for r in mates_of:
            stage[sweep, r, rows, :] = own[sweep][wanted[r], rows, :]
        for r in mates_of:
            to_mate(
                r, stage.at[sweep, r, rows], arrived.at[sweep, r, rows],
                far_send.at[SWEEPS if sweep == 0 and cuts[k][2] else sweep], far_recv.at[sweep, k],
            ).start()

    for copy in mine:
        copy.wait()
    pl.semaphore_wait(barrier, len(steps) + 2)

    for r in reversed(steps):
        to_mate(r, fblk_hbm, asked.at[r], ask_sem.at[0], ask_sem.at[r]).start()
    for k in early:
        c, w, via = cuts[k]
        to_mate(
            via, own[0].at[:, pl.ds(c, w)], pairs[k], pair_sem.at[len(early)], pair_sem.at[early.index(k)]
        ).start()
    for k in order:
        send_halo(0, k)
    for k, (c, w, _) in enumerate(cuts):
        for b in range(blocks):
            exts[0][k][1 + b] = own[0][b, pl.ds(c, w), :]
    for copy in words:
        copy.wait()

    for r in steps:
        to_mate(r, fblk_hbm, asked.at[r], ask_sem.at[0], ask_sem.at[r]).wait_recv()
    wanted = {r: asked[r, 0, me] for r in steps}
    for k in order:
        send_far(0, k, [r for r in reversed(steps) if not cuts[k][2] or r == 3 - cuts[k][2]])

    def weights(scaled):
        for b in range(blocks):
            for s in range(slots):
                part = band[b, s].astype(jnp.float32) * jnp.where(s < bcnt[b], 1.0, 0.0)
                if scaled:
                    part = part * scales[b + 1 + boff[b, s]][0:1, :]
                near_weights[b, pl.ds(s * tile, tile), :] = part.astype(jnp.bfloat16).T
        for r in range(peers):
            part = far[0, mates[r]]
            if scaled:
                row = far_scale_in[r] if r else own_scale[fblk[0, me]]
                part = (part.astype(jnp.float32) * row[0:1, :]).astype(jnp.bfloat16)
            part = part.T
            home = frow[0, mates[r]]
            for b in range(blocks):
                chosen = jnp.where(home == b, 1.0, 0.0).astype(jnp.bfloat16)
                far_weights[pl.ds(r * tile, tile), pl.ds(b * tile, tile)] = part * chosen

    band_load.wait()
    far_load.wait()
    weights(False)
    aff_load.wait()

    for i, k in enumerate(early):
        c, w, via = cuts[k]
        rows = pl.ds(c, w)
        over = 3 - via
        drain(pairs[k], pair_sem.at[i])
        stage[0, 3, rows, :] = pairs[k][asked[over, 0, mates[via]]]
        to_mate(
            over, stage.at[0, 3, rows], arrived.at[0, 3, rows], far_send.at[SWEEPS], far_recv.at[0, k]
        ).start()

    for sweep in range(SWEEPS):
        squares = jnp.zeros((1, blocks * tile), jnp.float32)
        for k in order:
            c, w, via = cuts[k]
            rows = pl.ds(c, w)
            drain(several(2, c, w), halo_recv.at[sweep, k])
            near = [
                jnp.dot(
                    jnp.concatenate(
                        [exts[sweep][k][b + 1 + boff[b, s]] for s in range(slots)], axis=1
                    ),
                    near_weights[b], preferred_element_type=jnp.float32,
                )
                for b in range(blocks)
            ]
            early_here = sweep == 0 and via
            drain(several(peers - 1 - (1 if early_here else 0), c, w), far_recv.at[sweep, k])
            parts = [own[sweep][fblk[0, me], rows, :]]
            for r in steps:
                if early_here and r == via:
                    parts.append(pairs[k][fblk[0, mates[r]]])
                else:
                    parts.append(arrived[sweep, r, rows, :])
            mixed = jnp.dot(
                jnp.concatenate(parts, axis=1), far_weights[...],
                preferred_element_type=jnp.float32,
            )
            mixed = mixed + jnp.concatenate(near, axis=1)
            mixed = propagation_weight * mixed + aff[rows, :].astype(jnp.float32)
            squares += jnp.sum(mixed * mixed, axis=0, keepdims=True)
            if sweep == SWEEPS - 1:
                acc[rows, :] = mixed
                continue
            for b in range(blocks):
                part = mixed[:, b * tile : (b + 1) * tile].astype(jnp.bfloat16)
                own[sweep + 1][b, rows, :] = part
                exts[sweep + 1][k][1 + b] = part
            send_far(sweep + 1, k, list(reversed(steps)))
            send_halo(sweep + 1, k)
        scale = lax.rsqrt(squares / classes + epsilon)
        if sweep == SWEEPS - 1:
            for c, w, _ in cuts:
                out[pl.ds(c, w), :] = (acc[pl.ds(c, w), :] * scale).astype(jnp.bfloat16)
            continue
        for b in range(blocks):
            own_scale[b] = jnp.broadcast_to(scale[:, b * tile : (b + 1) * tile], (8, tile))
            scales[1 + b] = own_scale[b]
        for r in steps:
            far_scale_out[r] = own_scale[wanted[r]]
        for r in reversed(steps):
            to_mate(
                r, far_scale_out.at[r], far_scale_in.at[r], scale_sem.at[0], scale_sem.at[1]
            ).start()
        to_sides(
            scales.at[1], scales.at[blocks], scales.at[0], scales.at[blocks + 1],
            scale_sem.at[0], scale_sem.at[1],
        )
        drain(scale_gauge, scale_sem.at[1])
        weights(True)

    for r in steps:
        to_mate(r, fblk_hbm, asked.at[r], ask_sem.at[0], ask_sem.at[r]).wait_send()
    relayed = sum(w for _, w, via in cuts if via)
    if early:
        drain(own[0].at[:, pl.ds(0, relayed)], pair_sem.at[len(early)])
        drain(several(2, 0, relayed), far_send.at[SWEEPS])
    drain(several(peers - 1, relayed, classes - relayed), far_send.at[0])
    drain(several(peers - 1, 0, classes), far_send.at[1])
    for sweep in range(SWEEPS):
        drain(several(2, 0, classes), halo_send.at[sweep])
    drain(scale_gauge, scale_sem.at[0])


def local(peers, ring, posterior, affinity, band_tiles, offset, count, far_tiles, far_row, far_block):
    rows, classes = posterior.shape
    blocks, slots, tile, _ = band_tiles.shape
    stored = pl.BlockSpec(memory_space=pltpu.HBM)
    kind = jnp.bfloat16
    cuts = chunks_of(classes, peers)
    pieces = len(cuts)
    early = sum(1 for cut in cuts if cut[2])
    scratch = [
        [pltpu.VMEM((blocks, classes, tile), kind)] * SWEEPS,
        [[pltpu.VMEM((blocks + 2, w, tile), kind) for _, w, _ in cuts] for _ in range(SWEEPS)],
        [pltpu.VMEM((blocks, w if via else 16, tile), kind) for _, w, via in cuts],
        pltpu.VMEM((SWEEPS, peers, classes, tile), kind),
        pltpu.VMEM((SWEEPS, peers, classes, tile), kind),
        pltpu.VMEM((max(peers - 1, 2), classes, tile), kind),
        pltpu.VMEM((peers + 1, 8, tile), jnp.float32),
        pltpu.SMEM((peers,) + far_block.shape, jnp.int32),
        pltpu.VMEM((classes, rows), kind),
        pltpu.VMEM(band_tiles.shape, kind),
        pltpu.VMEM(far_tiles.shape, kind),
        pltpu.VMEM((blocks, slots * tile, tile), kind),
        pltpu.VMEM((peers * tile, rows), kind),
        pltpu.VMEM((classes, rows), jnp.float32),
        pltpu.SMEM(offset.shape, jnp.int32),
        pltpu.SMEM(count.shape, jnp.int32),
        pltpu.SMEM(far_row.shape, jnp.int32),
        pltpu.SMEM(far_block.shape, jnp.int32),
        pltpu.VMEM((blocks + 2, 8, tile), jnp.float32),
        pltpu.VMEM((blocks, 8, tile), jnp.float32),
        pltpu.VMEM((peers, 8, tile), jnp.float32),
        pltpu.VMEM((peers, 8, tile), jnp.float32),
        pltpu.SemaphoreType.DMA((7 + blocks,)),
        pltpu.SemaphoreType.DMA((peers,)),
        pltpu.SemaphoreType.DMA((early + 1,)),
        pltpu.SemaphoreType.DMA((SWEEPS,)),
        pltpu.SemaphoreType.DMA((SWEEPS + 1,)),
        pltpu.SemaphoreType.DMA((SWEEPS, pieces)),
        pltpu.SemaphoreType.DMA((SWEEPS, pieces)),
        pltpu.SemaphoreType.DMA((2,)),
    ]
    held = min(8 * rows * classes * (3 + 2 * peers) + 24 * 2**20, 60 * 2**20)
    result = pl.pallas_call(
        functools.partial(kernel, peers, ring, cuts),
        out_shape=jax.ShapeDtypeStruct((classes, rows), kind),
        in_specs=[stored] * 8,
        out_specs=pl.BlockSpec(memory_space=pltpu.VMEM),
        scratch_shapes=scratch,
        compiler_params=pltpu.CompilerParams(
            collective_id=0, has_side_effects=True, vmem_limit_bytes=held
        ),
    )(
        *[
            pltpu.with_memory_space_constraint(value, pltpu.HBM)
            for value in (
                posterior.T, affinity.T, band_tiles, far_tiles, offset, count, far_row, far_block
            )
        ]
    )
    return result.T


def solution(mesh):
    spread = ("gx", "gy")
    in_specs = (
        P(spread, None), P(spread, None), P(spread, None, None, None), P(spread, None),
        P(spread), P(spread, None, None, None), P(spread, None), P(spread, None),
    )

    def run(posterior, affinity, band_tiles, offset, count, far_tiles, far_row, far_block):
        return local(
            mesh.shape["gx"], mesh.shape["gy"],
            posterior, affinity, band_tiles, offset, count, far_tiles, far_row, far_block,
        )

    return jax.shard_map(run, mesh=mesh, in_specs=in_specs, out_specs=P(spread, None), check_vma=False)
```

```python
import functools

import jax
import jax.numpy as jnp
from jax import lax
from jax.experimental import pallas as pl
from jax.experimental.pallas import tpu as pltpu
from jax.sharding import PartitionSpec as P

SWEEPS = 2
propagation_weight = 0.9
epsilon = 1e-06
SHARE = 0.32
HALVES = 1
DIRECT = 2
BRIDGE = 1
MESH = pl.DeviceIdType.MESH


def partner(me, step, peers):
    total = 0
    bit = 1
    while bit < peers:
        here = lax.rem(me // bit, 2)
        total = total + bit * (lax.rem(here + 1, 2) if step & bit else here)
        bit *= 2
    return total


def split(first, size, pieces):
    step = -(-size // (pieces * 16)) * 16
    return [(c, min(step, first + size - c)) for c in range(first, first + size, step)]


def chunks_of(classes, peers):
    cuts = []
    first = 0
    if peers == 4:
        share = int(classes * SHARE) // 16 * 16
        if share:
            for via in (1, 2):
                cuts += [(c, w, via) for c, w in split(first, share, HALVES)]
                first += share
    cuts += [(c, w, 0) for c, w in split(first, classes - first, DIRECT)]
    return cuts


def kernel(
    peers, ring, cuts,
    post, aff_hbm, band_hbm, far_hbm, boff_hbm, bcnt_hbm, frow_hbm, fblk_hbm,
    out,
    own, exts, raws, pairs, stage, arrived, gauge, scale_gauge, asked, aff, band, far, near_weights, far_weights, acc,
    boff, bcnt, frow, fblk, own_scale, far_scale_out, far_scale_in,
    load_sem, ask_sem, pair_sem, halo_send, far_send, halo_recv, far_recv, scale_sem, ready,
):
    me = lax.axis_index("gx")
    spot = lax.axis_index("gy")
    up = lax.rem(spot + 1, ring)
    down = lax.rem(spot + ring - 1, ring)
    blocks, slots, tile, _ = band.shape
    classes = post.shape[0]
    steps = list(range(1, peers))
    mates = {r: partner(me, r, peers) for r in range(peers)}
    order = list(range(len(cuts)))
    early = [k for k, cut in enumerate(cuts) if cut[2]]

    barrier = pltpu.get_barrier_semaphore()
    for r in steps:
        pl.semaphore_signal(barrier, inc=1, device_id={"gx": mates[r]}, device_id_type=MESH)

    def greet(sem, side, when):
        @pl.when(when)
        def _():
            pl.semaphore_signal(sem, inc=1, device_id={"gy": side}, device_id_type=MESH)

    greet(barrier, up, spot < ring - 1)
    greet(barrier, down, spot == 0)

    pending = []

    def load(source, target):
        copy = pltpu.make_async_copy(source, target, load_sem.at[len(pending)])
        copy.start()
        pending.append(copy)
        return copy

    mine = [load(post.at[:, pl.ds(b * tile, tile)], own[0].at[b]) for b in range(blocks)]
    words = [
        load(source, target)
        for source, target in ((fblk_hbm, fblk), (frow_hbm, frow), (bcnt_hbm, bcnt), (boff_hbm, boff))
    ]
    band_load = load(band_hbm, band)
    far_load = load(far_hbm, far)
    aff_load = load(aff_hbm, aff)

    def drain(whole, sem):
        pltpu.make_async_copy(whole, whole, sem).wait()

    def several(copies, first, size):
        return gauge.at[pl.ds(0, copies), pl.ds(first, size)]

    def to_mate(r, source, target, send, recv):
        return pltpu.make_async_remote_copy(
            src_ref=source, dst_ref=target, send_sem=send, recv_sem=recv,
            device_id={"gx": mates[r]}, device_id_type=MESH,
        )

    def to_sides(first, last, before, after, send, recv):
        for source, target, side in ((last, before, up), (first, after, down)):
            pltpu.make_async_remote_copy(
                src_ref=source, dst_ref=target, send_sem=send, recv_sem=recv,
                device_id={"gy": side}, device_id_type=MESH,
            ).start()

    def send_halo(sweep, k):
        c, w, _ = cuts[k]
        to_sides(
            own[sweep].at[0, pl.ds(c, w)], own[sweep].at[blocks - 1, pl.ds(c, w)],
            exts[sweep][k].at[0], exts[sweep][k].at[blocks + 1],
            halo_send.at[sweep], halo_recv.at[sweep, k],
        )

    def send_far(sweep, k, mates_of):
        c, w, _ = cuts[k]
        rows = pl.ds(c, w)
        for r in mates_of:
            if sweep and k < BRIDGE:
                stage[sweep, r, rows, :] = raws[k][wanted[r]]
            else:
                stage[sweep, r, rows, :] = own[sweep][wanted[r], rows, :]
        for r in mates_of:
            to_mate(
                r, stage.at[sweep, r, rows], arrived.at[sweep, r, rows],
                far_send.at[SWEEPS if sweep == 0 and cuts[k][2] else sweep], far_recv.at[sweep, k],
            ).start()

    for copy in mine:
        copy.wait()
    pl.semaphore_wait(
        barrier, len(steps) + jnp.where(spot == 0, 0, 1) + jnp.where(spot == ring - 1, 1, 0)
    )

    for r in reversed(steps):
        to_mate(r, fblk_hbm, asked.at[r], ask_sem.at[0], ask_sem.at[r]).start()
    for k in early:
        c, w, via = cuts[k]
        to_mate(
            via, own[0].at[:, pl.ds(c, w)], pairs[k], pair_sem.at[len(early)], pair_sem.at[early.index(k)]
        ).start()
    greet(ready.at[0], down, spot > 0)
    greet(ready.at[1], up, spot == ring - 1)
    for k, (c, w, _) in enumerate(cuts):
        for b in range(blocks):
            exts[0][k][1 + b] = own[0][b, pl.ds(c, w), :]
    for copy in words:
        copy.wait()
    for i, when in enumerate((spot < ring - 1, spot == 0)):
        @pl.when(when)
        def _():
            pl.semaphore_wait(ready.at[i], 1)
    for k in order:
        send_halo(0, k)

    for r in steps:
        to_mate(r, fblk_hbm, asked.at[r], ask_sem.at[0], ask_sem.at[r]).wait_recv()
    wanted = {r: asked[r, 0, me] for r in steps}
    for k in early:
        send_far(0, k, [3 - cuts[k][2]])

    def weights(scaled):
        if not scaled:
            for b in range(blocks):
                for s in range(slots):
                    part = band[b, s].astype(jnp.float32) * jnp.where(s < bcnt[b], 1.0, 0.0)
                    near_weights[b, pl.ds(s * tile, tile), :] = part.astype(jnp.bfloat16).T
        for r in range(peers):
            part = far[0, mates[r]]
            if scaled and r:
                part = (part.astype(jnp.float32) * far_scale_in[r][0:1, :]).astype(jnp.bfloat16)
            part = part.T
            home = frow[0, mates[r]]
            for b in range(blocks):
                chosen = jnp.where(home == b, 1.0, 0.0).astype(jnp.bfloat16)
                far_weights[scaled, pl.ds(r * tile, tile), pl.ds(b * tile, tile)] = part * chosen

    band_load.wait()
    far_load.wait()
    weights(0)
    aff_load.wait()

    for i, k in enumerate(early):
        c, w, via = cuts[k]
        rows = pl.ds(c, w)
        over = 3 - via
        drain(pairs[k], pair_sem.at[i])
        stage[0, 3, rows, :] = pairs[k][asked[over, 0, mates[via]]]
        to_mate(
            over, stage.at[0, 3, rows], arrived.at[0, 3, rows], far_send.at[SWEEPS], far_recv.at[0, k]
        ).start()
    for k in order:
        if k not in early:
            send_far(0, k, steps)

    def keep(sweep, k):
        c, w, _ = cuts[k]
        for b in range(blocks):
            value = acc[pl.ds(c, w), pl.ds(b * tile, tile)] * scale[:, b * tile : (b + 1) * tile]
            value = value.astype(jnp.bfloat16)
            own[sweep][b, pl.ds(c, w), :] = value
            exts[sweep][k][1 + b] = value

    for sweep in range(SWEEPS):
        squares = jnp.zeros((1, blocks * tile), jnp.float32)
        for k in order:
            c, w, via = cuts[k]
            rows = pl.ds(c, w)
            drain(several(2, c, w), halo_recv.at[sweep, k])
            near = [
                jnp.dot(
                    jnp.concatenate(
                        [exts[sweep][k][b + 1 + boff[b, s]] for s in range(slots)], axis=1
                    ),
                    near_weights[b], preferred_element_type=jnp.float32,
                )
                for b in range(blocks)
            ]
            early_here = sweep == 0 and via
            raw = sweep > 0 and k < BRIDGE
            if raw and k == 0:
                drain(scale_gauge, scale_sem.at[1])
                weights(1)
            drain(several(peers - 1 - (1 if early_here else 0), c, w), far_recv.at[sweep, k])
            parts = [own[sweep][fblk[0, me], rows, :]]
            for r in steps:
                if early_here and r == via:
                    parts.append(pairs[k][fblk[0, mates[r]]])
                else:
                    parts.append(arrived[sweep, r, rows, :])
            mixed = jnp.dot(
                jnp.concatenate(parts, axis=1), far_weights[1 if raw else 0],
                preferred_element_type=jnp.float32,
            )
            mixed = mixed + jnp.concatenate(near, axis=1)
            mixed = propagation_weight * mixed + aff[rows, :].astype(jnp.float32)
            squares += jnp.sum(mixed * mixed, axis=0, keepdims=True)
            acc[rows, :] = mixed
            if sweep < SWEEPS - 1 and k < BRIDGE:
                for b in range(blocks):
                    raws[k][b] = mixed[:, b * tile : (b + 1) * tile].astype(jnp.bfloat16)
                send_far(sweep + 1, k, steps)
        scale = lax.rsqrt(squares / classes + epsilon)
        if sweep == SWEEPS - 1:
            for c, w, _ in cuts:
                out[pl.ds(c, w), :] = (acc[pl.ds(c, w), :] * scale).astype(jnp.bfloat16)
            continue
        for b in range(blocks):
            own_scale[b] = jnp.broadcast_to(scale[:, b * tile : (b + 1) * tile], (8, tile))
        for r in steps:
            far_scale_out[r] = own_scale[wanted[r]]
        for r in steps:
            to_mate(
                r, far_scale_out.at[r], far_scale_in.at[r], scale_sem.at[0], scale_sem.at[1]
            ).start()
        for k in order[BRIDGE:]:
            keep(sweep + 1, k)
            send_far(sweep + 1, k, steps)
            if k == BRIDGE:
                for early_k in order[:BRIDGE]:
                    keep(sweep + 1, early_k)
                    send_halo(sweep + 1, early_k)
            send_halo(sweep + 1, k)

    for r in steps:
        to_mate(r, fblk_hbm, asked.at[r], ask_sem.at[0], ask_sem.at[r]).wait_send()
    relayed = sum(w for _, w, via in cuts if via)
    if early:
        drain(own[0].at[:, pl.ds(0, relayed)], pair_sem.at[len(early)])
        drain(several(2, 0, relayed), far_send.at[SWEEPS])
    drain(several(peers - 1, relayed, classes - relayed), far_send.at[0])
    drain(several(peers - 1, 0, classes), far_send.at[1])
    for sweep in range(SWEEPS):
        drain(several(2, 0, classes), halo_send.at[sweep])
    drain(scale_gauge, scale_sem.at[0])


def local(peers, ring, posterior, affinity, band_tiles, offset, count, far_tiles, far_row, far_block):
    rows, classes = posterior.shape
    blocks, slots, tile, _ = band_tiles.shape
    stored = pl.BlockSpec(memory_space=pltpu.HBM)
    kind = jnp.bfloat16
    cuts = chunks_of(classes, peers)
    pieces = len(cuts)
    early = sum(1 for cut in cuts if cut[2])
    scratch = [
        [pltpu.VMEM((blocks, classes, tile), kind)] * SWEEPS,
        [[pltpu.VMEM((blocks + 2, w, tile), kind) for _, w, _ in cuts] for _ in range(SWEEPS)],
        [pltpu.VMEM((blocks, w, tile), kind) for _, w, _ in cuts[:BRIDGE]],
        [pltpu.VMEM((blocks, w if via else 16, tile), kind) for _, w, via in cuts],
        pltpu.VMEM((SWEEPS, peers, classes, tile), kind),
        pltpu.VMEM((SWEEPS, peers, classes, tile), kind),
        pltpu.VMEM((max(peers - 1, 2), classes, tile), kind),
        pltpu.VMEM((peers - 1, 8, tile), jnp.float32),
        pltpu.SMEM((peers,) + far_block.shape, jnp.int32),
        pltpu.VMEM((classes, rows), kind),
        pltpu.VMEM(band_tiles.shape, kind),
        pltpu.VMEM(far_tiles.shape, kind),
        pltpu.VMEM((blocks, slots * tile, tile), kind),
        pltpu.VMEM((2, peers * tile, rows), kind),
        pltpu.VMEM((classes, rows), jnp.float32),
        pltpu.SMEM(offset.shape, jnp.int32),
        pltpu.SMEM(count.shape, jnp.int32),
        pltpu.SMEM(far_row.shape, jnp.int32),
        pltpu.SMEM(far_block.shape, jnp.int32),
        pltpu.VMEM((blocks, 8, tile), jnp.float32),
        pltpu.VMEM((peers, 8, tile), jnp.float32),
        pltpu.VMEM((peers, 8, tile), jnp.float32),
        pltpu.SemaphoreType.DMA((7 + blocks,)),
        pltpu.SemaphoreType.DMA((peers,)),
        pltpu.SemaphoreType.DMA((early + 1,)),
        pltpu.SemaphoreType.DMA((SWEEPS,)),
        pltpu.SemaphoreType.DMA((SWEEPS + 1,)),
        pltpu.SemaphoreType.DMA((SWEEPS, pieces)),
        pltpu.SemaphoreType.DMA((SWEEPS, pieces)),
        pltpu.SemaphoreType.DMA((2,)),
        pltpu.SemaphoreType.REGULAR((2,)),
    ]
    held = min(8 * rows * classes * (3 + 2 * peers) + 24 * 2**20, 60 * 2**20)
    result = pl.pallas_call(
        functools.partial(kernel, peers, ring, cuts),
        out_shape=jax.ShapeDtypeStruct((classes, rows), kind),
        in_specs=[stored] * 8,
        out_specs=pl.BlockSpec(memory_space=pltpu.VMEM),
        scratch_shapes=scratch,
        compiler_params=pltpu.CompilerParams(
            collective_id=0, has_side_effects=True, vmem_limit_bytes=held
        ),
    )(
        *[
            pltpu.with_memory_space_constraint(value, pltpu.HBM)
            for value in (
                posterior.T, affinity.T, band_tiles, far_tiles, offset, count, far_row, far_block
            )
        ]
    )
    return result.T


def solution(mesh):
    spread = ("gx", "gy")
    in_specs = (
        P(spread, None), P(spread, None), P(spread, None, None, None), P(spread, None),
        P(spread), P(spread, None, None, None), P(spread, None), P(spread, None),
    )

    def run(posterior, affinity, band_tiles, offset, count, far_tiles, far_row, far_block):
        return local(
            mesh.shape["gx"], mesh.shape["gy"],
            posterior, affinity, band_tiles, offset, count, far_tiles, far_row, far_block,
        )

    return jax.shard_map(run, mesh=mesh, in_specs=in_specs, out_specs=P(spread, None), check_vma=False)
```

```python
import functools

import jax
import jax.numpy as jnp
from jax import lax
from jax.experimental import pallas as pl
from jax.experimental.pallas import tpu as pltpu
from jax.sharding import PartitionSpec as P

SWEEPS = 2
propagation_weight = 0.9
epsilon = 1e-06
SHARE = 0.38
HALVES = 1
DIRECT = 1
BRIDGE = 1
MESH = pl.DeviceIdType.MESH


def partner(me, step, peers):
    total = 0
    bit = 1
    while bit < peers:
        here = lax.rem(me // bit, 2)
        total = total + bit * (lax.rem(here + 1, 2) if step & bit else here)
        bit *= 2
    return total


def split(first, size, pieces):
    step = -(-size // (pieces * 16)) * 16
    return [(c, min(step, first + size - c)) for c in range(first, first + size, step)]


def chunks_of(classes, peers):
    cuts = []
    first = 0
    if peers == 4:
        share = int(classes * SHARE) // 16 * 16
        if share:
            for via in (1, 2):
                cuts += [(c, w, via) for c, w in split(first, share, HALVES)]
                first += share
    cuts += [(c, w, 0) for c, w in split(first, classes - first, DIRECT)]
    return cuts


def kernel(
    peers, ring, cuts,
    post, aff_hbm, band_hbm, far_hbm, boff_hbm, bcnt_hbm, frow_hbm, fblk_hbm,
    out,
    own, exts, raws, pairs, stage, arrived, gauge, scale_gauge, asked, aff, band, far, near_weights, far_weights, acc,
    boff, bcnt, frow, fblk, own_scale, far_scale_out, far_scale_in,
    local_sem, ask_sem, pair_sem, halo_recv, far_recv, scale_sem, ready,
):
    me = lax.axis_index("gx")
    spot = lax.axis_index("gy")
    up = lax.rem(spot + 1, ring)
    down = lax.rem(spot + ring - 1, ring)
    blocks, slots, tile, _ = band.shape
    classes = post.shape[0]
    steps = sorted(range(1, peers), key=lambda r: (-bin(r).count("1"), r))
    mates = {r: partner(me, r, peers) for r in range(peers)}
    order = list(range(len(cuts)))
    early = [k for k, cut in enumerate(cuts) if cut[2]]

    barrier = pltpu.get_barrier_semaphore()
    for r in steps:
        pl.semaphore_signal(barrier, inc=1, device_id={"gx": mates[r]}, device_id_type=MESH)

    def greet(sem, side, when):
        @pl.when(when)
        def _():
            pl.semaphore_signal(sem, inc=1, device_id={"gy": side}, device_id_type=MESH)

    greet(barrier, up, spot < ring - 1)
    greet(barrier, down, spot == 0)

    pending = []
    pair_send, halo_send, far_send, scale_send = (
        local_sem.at[0], [local_sem.at[1], local_sem.at[2]],
        [local_sem.at[3], local_sem.at[6], local_sem.at[4]], local_sem.at[5],
    )

    def load(source, target):
        copy = pltpu.make_async_copy(source, target, local_sem.at[len(pending)])
        copy.start()
        pending.append(copy)
        return copy

    for b in range(blocks):
        pltpu.make_async_copy(post.at[:, pl.ds(b * tile, tile)], own[0].at[b], local_sem.at[0]).start()
    pending.append(None)
    words = [
        load(source, target)
        for source, target in ((fblk_hbm, fblk), (frow_hbm, frow), (bcnt_hbm, bcnt), (boff_hbm, boff))
    ]
    band_load = load(band_hbm, band)
    far_load = load(far_hbm, far)
    aff_load = load(aff_hbm, aff)

    def drain(whole, sem):
        pltpu.make_async_copy(whole, whole, sem).wait()

    def several(copies, first, size):
        return gauge.at[pl.ds(0, copies), pl.ds(first, size)]

    def to_mate(r, source, target, send, recv):
        return pltpu.make_async_remote_copy(
            src_ref=source, dst_ref=target, send_sem=send, recv_sem=recv,
            device_id={"gx": mates[r]}, device_id_type=MESH,
        )

    def to_sides(first, last, before, after, send, recv):
        for source, target, side in ((last, before, up), (first, after, down)):
            pltpu.make_async_remote_copy(
                src_ref=source, dst_ref=target, send_sem=send, recv_sem=recv,
                device_id={"gy": side}, device_id_type=MESH,
            ).start()

    def flock(sweep, k):
        return sweep + 1 if sweep else min(k, 1)

    def send_halo(sweep, k):
        c, w, _ = cuts[k]
        to_sides(
            own[sweep].at[0, pl.ds(c, w)], own[sweep].at[blocks - 1, pl.ds(c, w)],
            exts[sweep][k].at[0], exts[sweep][k].at[blocks + 1],
            halo_send[sweep], halo_recv.at[flock(sweep, k)],
        )

    def send_far(sweep, k, mates_of):
        c, w, _ = cuts[k]
        rows = pl.ds(c, w)
        for r in mates_of:
            if sweep and k < BRIDGE:
                stage[sweep, r, rows, :] = raws[k][wanted[r]]
            else:
                stage[sweep, r, rows, :] = own[sweep][wanted[r], rows, :]
        for r in mates_of:
            to_mate(
                r, stage.at[sweep, r, rows], arrived.at[sweep, r, rows],
                far_send[SWEEPS if sweep == 0 and cuts[k][2] else sweep], far_recv.at[sweep, k],
            ).start()

    drain(own[0], local_sem.at[0])
    pl.semaphore_wait(
        barrier, len(steps) + jnp.where(spot == 0, 0, 1) + jnp.where(spot == ring - 1, 1, 0)
    )

    for r in reversed(steps):
        to_mate(r, fblk_hbm, asked.at[r], ask_sem.at[0], ask_sem.at[r]).start()
    for k in early:
        c, w, via = cuts[k]
        to_mate(
            via, own[0].at[:, pl.ds(c, w)], pairs[k], pair_send, pair_sem.at[early.index(k)]
        ).start()
    greet(ready.at[0], down, spot > 0)
    greet(ready.at[1], up, spot == ring - 1)
    for k, (c, w, _) in enumerate(cuts):
        for b in range(blocks):
            exts[0][k][1 + b] = own[0][b, pl.ds(c, w), :]
    for copy in words:
        copy.wait()
    for i, when in enumerate((spot < ring - 1, spot == 0)):
        @pl.when(when)
        def _():
            pl.semaphore_wait(ready.at[i], 1)
    for k in order:
        send_halo(0, k)

    wanted = {}

    def hear(mates_of):
        for r in mates_of:
            to_mate(r, fblk_hbm, asked.at[r], ask_sem.at[0], ask_sem.at[r]).wait_recv()
            wanted[r] = asked[r, 0, me]

    near_mates = [r for r in steps if r & (r - 1) == 0]
    hear(near_mates)
    for k in early:
        send_far(0, k, [3 - cuts[k][2]])

    def weights(scaled):
        if not scaled:
            for b in range(blocks):
                for s in range(slots):
                    part = band[b, s].astype(jnp.float32) * jnp.where(s < bcnt[b], 1.0, 0.0)
                    near_weights[b, pl.ds(s * tile, tile), :] = part.astype(jnp.bfloat16).T
        for r in range(peers):
            part = far[0, mates[r]]
            if scaled and r:
                part = (part.astype(jnp.float32) * far_scale_in[r][0:1, :]).astype(jnp.bfloat16)
            part = part.T
            home = frow[0, mates[r]]
            for b in range(blocks):
                chosen = jnp.where(home == b, 1.0, 0.0).astype(jnp.bfloat16)
                far_weights[scaled, pl.ds(r * tile, tile), pl.ds(b * tile, tile)] = part * chosen

    band_load.wait()
    far_load.wait()
    weights(0)
    aff_load.wait()

    for i, k in enumerate(early):
        c, w, via = cuts[k]
        rows = pl.ds(c, w)
        over = 3 - via
        drain(pairs[k], pair_sem.at[i])
        stage[0, 3, rows, :] = pairs[k][asked[over, 0, mates[via]]]
        to_mate(
            over, stage.at[0, 3, rows], arrived.at[0, 3, rows], far_send[SWEEPS], far_recv.at[0, k]
        ).start()
    hear([r for r in steps if r not in near_mates])
    for k in order:
        if k not in early:
            send_far(0, k, steps)

    def keep(sweep, k):
        c, w, _ = cuts[k]
        for b in range(blocks):
            value = acc[pl.ds(c, w), pl.ds(b * tile, tile)] * scale[:, b * tile : (b + 1) * tile]
            value = value.astype(jnp.bfloat16)
            own[sweep][b, pl.ds(c, w), :] = value
            exts[sweep][k][1 + b] = value

    for sweep in range(SWEEPS):
        squares = jnp.zeros((1, blocks * tile), jnp.float32)
        for k in order:
            c, w, via = cuts[k]
            rows = pl.ds(c, w)
            if sweep == 0 and k == 0:
                drain(several(2, c, w), halo_recv.at[0])
            if sweep == 0 and k == 1:
                drain(several(2, c, classes - c), halo_recv.at[1])
            if sweep > 0 and k == 0:
                drain(several(2, 0, classes), halo_recv.at[2])
            near = [
                jnp.dot(
                    jnp.concatenate(
                        [exts[sweep][k][b + 1 + boff[b, s]] for s in range(slots)], axis=1
                    ),
                    near_weights[b], preferred_element_type=jnp.float32,
                )
                for b in range(blocks)
            ]
            early_here = sweep == 0 and via
            raw = sweep > 0 and k < BRIDGE
            if raw and k == 0:
                drain(scale_gauge, scale_sem.at[0])
                weights(1)
            drain(several(peers - 1 - (1 if early_here else 0), c, w), far_recv.at[sweep, k])
            parts = [own[sweep][fblk[0, me], rows, :]]
            for r in range(1, peers):
                if early_here and r == via:
                    parts.append(pairs[k][fblk[0, mates[r]]])
                else:
                    parts.append(arrived[sweep, r, rows, :])
            mixed = jnp.dot(
                jnp.concatenate(parts, axis=1), far_weights[1 if raw else 0],
                preferred_element_type=jnp.float32,
            )
            mixed = mixed + jnp.concatenate(near, axis=1)
            mixed = propagation_weight * mixed + aff[rows, :].astype(jnp.float32)
            squares += jnp.sum(mixed * mixed, axis=0, keepdims=True)
            acc[rows, :] = mixed
            if sweep < SWEEPS - 1 and k < BRIDGE:
                for b in range(blocks):
                    raws[k][b] = mixed[:, b * tile : (b + 1) * tile].astype(jnp.bfloat16)
                send_far(sweep + 1, k, steps)
        scale = lax.rsqrt(squares / classes + epsilon)
        if sweep == SWEEPS - 1:
            for c, w, _ in cuts:
                out[pl.ds(c, w), :] = (acc[pl.ds(c, w), :] * scale).astype(jnp.bfloat16)
            continue
        for b in range(blocks):
            own_scale[b] = jnp.broadcast_to(scale[:, b * tile : (b + 1) * tile], (8, tile))
        for r in steps:
            far_scale_out[r] = own_scale[wanted[r]]
        for r in steps:
            to_mate(
                r, far_scale_out.at[r], far_scale_in.at[r], scale_send, scale_sem.at[0]
            ).start()
        for k in order[BRIDGE:]:
            keep(sweep + 1, k)
            send_far(sweep + 1, k, steps)
            if k == BRIDGE:
                for early_k in order[:BRIDGE]:
                    keep(sweep + 1, early_k)
                    send_halo(sweep + 1, early_k)
            send_halo(sweep + 1, k)

    for r in steps:
        to_mate(r, fblk_hbm, asked.at[r], ask_sem.at[0], ask_sem.at[r]).wait_send()
    relayed = sum(w for _, w, via in cuts if via)
    if early:
        drain(own[0].at[:, pl.ds(0, relayed)], pair_send)
        drain(several(2, 0, relayed), far_send[SWEEPS])
    drain(several(peers - 1, relayed, classes - relayed), far_send[0])
    drain(several(peers - 1, 0, classes), far_send[1])
    for sweep in range(SWEEPS):
        drain(several(2, 0, classes), halo_send[sweep])
    drain(scale_gauge, scale_send)


def local(peers, ring, posterior, affinity, band_tiles, offset, count, far_tiles, far_row, far_block):
    rows, classes = posterior.shape
    blocks, slots, tile, _ = band_tiles.shape
    stored = pl.BlockSpec(memory_space=pltpu.HBM)
    kind = jnp.bfloat16
    cuts = chunks_of(classes, peers)
    pieces = len(cuts)
    early = sum(1 for cut in cuts if cut[2])
    scratch = [
        [pltpu.VMEM((blocks, classes, tile), kind)] * SWEEPS,
        [[pltpu.VMEM((blocks + 2, w, tile), kind) for _, w, _ in cuts] for _ in range(SWEEPS)],
        [pltpu.VMEM((blocks, w, tile), kind) for _, w, _ in cuts[:BRIDGE]],
        [pltpu.VMEM((blocks, w if via else 16, tile), kind) for _, w, via in cuts],
        pltpu.VMEM((SWEEPS, peers, classes, tile), kind),
        pltpu.VMEM((SWEEPS, peers, classes, tile), kind),
        pltpu.VMEM((max(peers - 1, 2), classes, tile), kind),
        pltpu.VMEM((peers - 1, 8, tile), jnp.float32),
        pltpu.SMEM((peers,) + far_block.shape, jnp.int32),
        pltpu.VMEM((classes, rows), kind),
        pltpu.VMEM(band_tiles.shape, kind),
        pltpu.VMEM(far_tiles.shape, kind),
        pltpu.VMEM((blocks, slots * tile, tile), kind),
        pltpu.VMEM((2, peers * tile, rows), kind),
        pltpu.VMEM((classes, rows), jnp.float32),
        pltpu.SMEM(offset.shape, jnp.int32),
        pltpu.SMEM(count.shape, jnp.int32),
        pltpu.SMEM(far_row.shape, jnp.int32),
        pltpu.SMEM(far_block.shape, jnp.int32),
        pltpu.VMEM((blocks, 8, tile), jnp.float32),
        pltpu.VMEM((peers, 8, tile), jnp.float32),
        pltpu.VMEM((peers, 8, tile), jnp.float32),
        pltpu.SemaphoreType.DMA((8,)),
        pltpu.SemaphoreType.DMA((peers,)),
        pltpu.SemaphoreType.DMA((max(early, 1),)),
        pltpu.SemaphoreType.DMA((SWEEPS + 1,)),
        pltpu.SemaphoreType.DMA((SWEEPS, pieces)),
        pltpu.SemaphoreType.DMA((1,)),
        pltpu.SemaphoreType.REGULAR((2,)),
    ]
    held = min(8 * rows * classes * (3 + 2 * peers) + 24 * 2**20, 60 * 2**20)
    result = pl.pallas_call(
        functools.partial(kernel, peers, ring, cuts),
        out_shape=jax.ShapeDtypeStruct((classes, rows), kind),
        in_specs=[stored] * 8,
        out_specs=pl.BlockSpec(memory_space=pltpu.VMEM),
        scratch_shapes=scratch,
        compiler_params=pltpu.CompilerParams(
            collective_id=0, has_side_effects=True, vmem_limit_bytes=held
        ),
    )(
        *[
            pltpu.with_memory_space_constraint(value, pltpu.HBM)
            for value in (
                posterior.T, affinity.T, band_tiles, far_tiles, offset, count, far_row, far_block
            )
        ]
    )
    return result.T


def solution(mesh):
    spread = ("gx", "gy")
    in_specs = (
        P(spread, None), P(spread, None), P(spread, None, None, None), P(spread, None),
        P(spread), P(spread, None, None, None), P(spread, None), P(spread, None),
    )

    def run(posterior, affinity, band_tiles, offset, count, far_tiles, far_row, far_block):
        return local(
            mesh.shape["gx"], mesh.shape["gy"],
            posterior, affinity, band_tiles, offset, count, far_tiles, far_row, far_block,
        )

    return jax.shard_map(run, mesh=mesh, in_specs=in_specs, out_specs=P(spread, None), check_vma=False)
```

```python
import functools

import jax
import jax.numpy as jnp
from jax import lax
from jax.experimental import pallas as pl
from jax.experimental.pallas import tpu as pltpu
from jax.sharding import PartitionSpec as P

SWEEPS = 2
propagation_weight = 0.9
epsilon = 1e-06
SHARE = 0.352
HALVES = 1
DIRECT = 1
BRIDGE = 1
MESH = pl.DeviceIdType.MESH


def partner(me, step, peers):
    total = 0
    bit = 1
    while bit < peers:
        here = lax.rem(me // bit, 2)
        total = total + bit * (lax.rem(here + 1, 2) if step & bit else here)
        bit *= 2
    return total


def split(first, size, pieces):
    step = -(-size // (pieces * 16)) * 16
    return [(c, min(step, first + size - c)) for c in range(first, first + size, step)]


def chunks_of(classes, peers):
    cuts = []
    first = 0
    if peers == 4:
        share = int(classes * SHARE) // 16 * 16
        if share:
            for via in (1, 2):
                cuts += [(c, w, via) for c, w in split(first, share, HALVES)]
                first += share
    cuts += [(c, w, 0) for c, w in split(first, classes - first, DIRECT)]
    return cuts


def kernel(
    peers, ring, cuts,
    post, aff_hbm, band_hbm, far_hbm, boff_hbm, bcnt_hbm, frow_hbm, fblk_hbm,
    out,
    own, exts, raws, pairs, stage, arrived, gauge, scale_gauge, asked, aff, band, far, near_weights, far_weights, acc,
    boff, bcnt, frow, fblk, own_scale, far_scale_out, far_scale_in,
    local_sem, ask_sem, pair_sem, halo_recv, far_recv, scale_sem, ready,
):
    me = lax.axis_index("gx")
    spot = lax.axis_index("gy")
    up = lax.rem(spot + 1, ring)
    down = lax.rem(spot + ring - 1, ring)
    blocks, slots, tile, _ = band.shape
    classes = post.shape[0]
    steps = sorted(range(1, peers), key=lambda r: (-bin(r).count("1"), r))
    mates = {r: partner(me, r, peers) for r in range(peers)}
    order = list(range(len(cuts)))
    early = [k for k, cut in enumerate(cuts) if cut[2]]

    barrier = pltpu.get_barrier_semaphore()
    for r in steps:
        pl.semaphore_signal(barrier, inc=1, device_id={"gx": mates[r]}, device_id_type=MESH)

    def greet(sem, side, when):
        @pl.when(when)
        def _():
            pl.semaphore_signal(sem, inc=1, device_id={"gy": side}, device_id_type=MESH)

    greet(barrier, up, spot < ring - 1)
    greet(barrier, down, spot == 0)

    pending = []
    pair_send, halo_send, far_send, scale_send = (
        local_sem.at[0], [local_sem.at[1], local_sem.at[2]],
        [local_sem.at[3], local_sem.at[6], local_sem.at[4]], local_sem.at[5],
    )

    def load(source, target):
        copy = pltpu.make_async_copy(source, target, local_sem.at[len(pending)])
        copy.start()
        pending.append(copy)
        return copy

    for b in range(blocks):
        pltpu.make_async_copy(post.at[:, pl.ds(b * tile, tile)], own[0].at[b], local_sem.at[0]).start()
    pending.append(None)
    words = [
        load(source, target)
        for source, target in ((fblk_hbm, fblk), (frow_hbm, frow), (bcnt_hbm, bcnt), (boff_hbm, boff))
    ]
    band_load = load(band_hbm, band)
    far_load = load(far_hbm, far)
    aff_load = load(aff_hbm, aff)

    def drain(whole, sem):
        pltpu.make_async_copy(whole, whole, sem).wait()

    def several(copies, first, size):
        return gauge.at[pl.ds(0, copies), pl.ds(first, size)]

    def to_mate(r, source, target, send, recv):
        return pltpu.make_async_remote_copy(
            src_ref=source, dst_ref=target, send_sem=send, recv_sem=recv,
            device_id={"gx": mates[r]}, device_id_type=MESH,
        )

    def to_sides(first, last, before, after, send, recv):
        for source, target, side in ((last, before, up), (first, after, down)):
            pltpu.make_async_remote_copy(
                src_ref=source, dst_ref=target, send_sem=send, recv_sem=recv,
                device_id={"gy": side}, device_id_type=MESH,
            ).start()

    def flock(sweep, k):
        return sweep + 1 if sweep else min(k, 1)

    def send_halo(sweep, k):
        c, w, _ = cuts[k]
        to_sides(
            own[sweep].at[0, pl.ds(c, w)], own[sweep].at[blocks - 1, pl.ds(c, w)],
            exts[sweep][k].at[0], exts[sweep][k].at[blocks + 1],
            halo_send[sweep], halo_recv.at[flock(sweep, k)],
        )

    def send_far(sweep, k, mates_of):
        c, w, _ = cuts[k]
        rows = pl.ds(c, w)
        for r in mates_of:
            if sweep and k < BRIDGE:
                stage[sweep, r, rows, :] = raws[k][wanted[r]]
            else:
                stage[sweep, r, rows, :] = own[sweep][wanted[r], rows, :]
            to_mate(
                r, stage.at[sweep, r, rows], arrived.at[sweep, r, rows],
                far_send[SWEEPS if sweep == 0 and cuts[k][2] else sweep], far_recv.at[sweep, k],
            ).start()

    drain(own[0], local_sem.at[0])
    pl.semaphore_wait(
        barrier, len(steps) + jnp.where(spot == 0, 0, 1) + jnp.where(spot == ring - 1, 1, 0)
    )

    for r in reversed(steps):
        to_mate(r, fblk_hbm, asked.at[r], ask_sem.at[0], ask_sem.at[r]).start()
    for k in early:
        c, w, via = cuts[k]
        to_mate(
            via, own[0].at[:, pl.ds(c, w)], pairs[k], pair_send, pair_sem.at[early.index(k)]
        ).start()
    greet(ready.at[0], down, spot > 0)
    greet(ready.at[1], up, spot == ring - 1)
    for k, (c, w, _) in enumerate(cuts):
        for b in range(blocks):
            exts[0][k][1 + b] = own[0][b, pl.ds(c, w), :]
    for copy in words:
        copy.wait()
    for i, when in enumerate((spot < ring - 1, spot == 0)):
        @pl.when(when)
        def _():
            pl.semaphore_wait(ready.at[i], 1)
    for k in order:
        send_halo(0, k)

    wanted = {}

    def hear(mates_of):
        for r in mates_of:
            to_mate(r, fblk_hbm, asked.at[r], ask_sem.at[0], ask_sem.at[r]).wait_recv()
            wanted[r] = asked[r, 0, me]

    near_mates = [r for r in steps if r & (r - 1) == 0]
    hear(near_mates)
    for k in early:
        send_far(0, k, [3 - cuts[k][2]])

    def weights(scaled):
        if not scaled:
            for b in range(blocks):
                for s in range(slots):
                    part = band[b, s].astype(jnp.float32) * jnp.where(s < bcnt[b], 1.0, 0.0)
                    near_weights[b, pl.ds(s * tile, tile), :] = part.astype(jnp.bfloat16).T
        for r in range(peers):
            part = far[0, mates[r]]
            if scaled and r:
                part = (part.astype(jnp.float32) * far_scale_in[r][0:1, :]).astype(jnp.bfloat16)
            part = part.T
            home = frow[0, mates[r]]
            for b in range(blocks):
                chosen = jnp.where(home == b, 1.0, 0.0).astype(jnp.bfloat16)
                far_weights[scaled, pl.ds(r * tile, tile), pl.ds(b * tile, tile)] = part * chosen

    band_load.wait()
    far_load.wait()
    weights(0)
    hear([r for r in steps if r not in near_mates])
    for k in order:
        if k not in early:
            send_far(0, k, [r for r in steps if r not in near_mates])
    aff_load.wait()

    for i, k in enumerate(early):
        c, w, via = cuts[k]
        rows = pl.ds(c, w)
        over = 3 - via
        drain(pairs[k], pair_sem.at[i])
        stage[0, 3, rows, :] = pairs[k][asked[over, 0, mates[via]]]
        to_mate(
            over, stage.at[0, 3, rows], arrived.at[0, 3, rows], far_send[SWEEPS], far_recv.at[0, k]
        ).start()
    for k in order:
        if k not in early:
            send_far(0, k, [r for r in steps if r in near_mates])

    def keep(sweep, k):
        c, w, _ = cuts[k]
        for b in range(blocks):
            value = acc[pl.ds(c, w), pl.ds(b * tile, tile)] * scale[:, b * tile : (b + 1) * tile]
            value = value.astype(jnp.bfloat16)
            own[sweep][b, pl.ds(c, w), :] = value
            exts[sweep][k][1 + b] = value

    for sweep in range(SWEEPS):
        squares = jnp.zeros((1, blocks * tile), jnp.float32)
        for k in order:
            c, w, via = cuts[k]
            rows = pl.ds(c, w)
            if sweep == 0 and k == 0:
                drain(several(2, c, w), halo_recv.at[0])
            if sweep == 0 and k == 1:
                drain(several(2, c, classes - c), halo_recv.at[1])
            if sweep > 0 and k == 0:
                drain(several(2, 0, classes), halo_recv.at[2])
            near = [
                jnp.dot(
                    jnp.concatenate(
                        [exts[sweep][k][b + 1 + boff[b, s]] for s in range(slots)], axis=1
                    ),
                    near_weights[b], preferred_element_type=jnp.float32,
                )
                for b in range(blocks)
            ]
            early_here = sweep == 0 and via
            raw = sweep > 0 and k < BRIDGE
            if raw and k == 0:
                drain(scale_gauge, scale_sem.at[0])
                weights(1)
            drain(several(peers - 1 - (1 if early_here else 0), c, w), far_recv.at[sweep, k])
            parts = [own[sweep][fblk[0, me], rows, :]]
            for r in range(1, peers):
                if early_here and r == via:
                    parts.append(pairs[k][fblk[0, mates[r]]])
                else:
                    parts.append(arrived[sweep, r, rows, :])
            mixed = jnp.dot(
                jnp.concatenate(parts, axis=1), far_weights[1 if raw else 0],
                preferred_element_type=jnp.float32,
            )
            mixed = mixed + jnp.concatenate(near, axis=1)
            mixed = propagation_weight * mixed + aff[rows, :].astype(jnp.float32)
            squares += jnp.sum(mixed * mixed, axis=0, keepdims=True)
            acc[rows, :] = mixed
            if sweep < SWEEPS - 1 and k < BRIDGE:
                for b in range(blocks):
                    raws[k][b] = mixed[:, b * tile : (b + 1) * tile].astype(jnp.bfloat16)
                send_far(sweep + 1, k, steps)
        scale = lax.rsqrt(squares / classes + epsilon)
        if sweep == SWEEPS - 1:
            for c, w, _ in cuts:
                out[pl.ds(c, w), :] = (acc[pl.ds(c, w), :] * scale).astype(jnp.bfloat16)
            continue
        for b in range(blocks):
            own_scale[b] = jnp.broadcast_to(scale[:, b * tile : (b + 1) * tile], (8, tile))
        for r in steps:
            far_scale_out[r] = own_scale[wanted[r]]
        for r in steps:
            to_mate(
                r, far_scale_out.at[r], far_scale_in.at[r], scale_send, scale_sem.at[0]
            ).start()
        for k in order:
            keep(sweep + 1, k)
            send_halo(sweep + 1, k)
            if k >= BRIDGE:
                send_far(sweep + 1, k, steps)

    for r in steps:
        to_mate(r, fblk_hbm, asked.at[r], ask_sem.at[0], ask_sem.at[r]).wait_send()
    relayed = sum(w for _, w, via in cuts if via)
    if early:
        drain(own[0].at[:, pl.ds(0, relayed)], pair_send)
        drain(several(2, 0, relayed), far_send[SWEEPS])
    drain(several(peers - 1, relayed, classes - relayed), far_send[0])
    drain(several(peers - 1, 0, classes), far_send[1])
    for sweep in range(SWEEPS):
        drain(several(2, 0, classes), halo_send[sweep])
    drain(scale_gauge, scale_send)


def local(peers, ring, posterior, affinity, band_tiles, offset, count, far_tiles, far_row, far_block):
    rows, classes = posterior.shape
    blocks, slots, tile, _ = band_tiles.shape
    stored = pl.BlockSpec(memory_space=pltpu.HBM)
    kind = jnp.bfloat16
    cuts = chunks_of(classes, peers)
    pieces = len(cuts)
    early = sum(1 for cut in cuts if cut[2])
    scratch = [
        [pltpu.VMEM((blocks, classes, tile), kind)] * SWEEPS,
        [[pltpu.VMEM((blocks + 2, w, tile), kind) for _, w, _ in cuts] for _ in range(SWEEPS)],
        [pltpu.VMEM((blocks, w, tile), kind) for _, w, _ in cuts[:BRIDGE]],
        [pltpu.VMEM((blocks, w if via else 16, tile), kind) for _, w, via in cuts],
        pltpu.VMEM((SWEEPS, peers, classes, tile), kind),
        pltpu.VMEM((SWEEPS, peers, classes, tile), kind),
        pltpu.VMEM((max(peers - 1, 2), classes, tile), kind),
        pltpu.VMEM((peers - 1, 8, tile), jnp.float32),
        pltpu.SMEM((peers,) + far_block.shape, jnp.int32),
        pltpu.VMEM((classes, rows), kind),
        pltpu.VMEM(band_tiles.shape, kind),
        pltpu.VMEM(far_tiles.shape, kind),
        pltpu.VMEM((blocks, slots * tile, tile), kind),
        pltpu.VMEM((2, peers * tile, rows), kind),
        pltpu.VMEM((classes, rows), jnp.float32),
        pltpu.SMEM(offset.shape, jnp.int32),
        pltpu.SMEM(count.shape, jnp.int32),
        pltpu.SMEM(far_row.shape, jnp.int32),
        pltpu.SMEM(far_block.shape, jnp.int32),
        pltpu.VMEM((blocks, 8, tile), jnp.float32),
        pltpu.VMEM((peers, 8, tile), jnp.float32),
        pltpu.VMEM((peers, 8, tile), jnp.float32),
        pltpu.SemaphoreType.DMA((8,)),
        pltpu.SemaphoreType.DMA((peers,)),
        pltpu.SemaphoreType.DMA((max(early, 1),)),
        pltpu.SemaphoreType.DMA((SWEEPS + 1,)),
        pltpu.SemaphoreType.DMA((SWEEPS, pieces)),
        pltpu.SemaphoreType.DMA((1,)),
        pltpu.SemaphoreType.REGULAR((2,)),
    ]
    held = min(8 * rows * classes * (3 + 2 * peers) + 24 * 2**20, 60 * 2**20)
    result = pl.pallas_call(
        functools.partial(kernel, peers, ring, cuts),
        out_shape=jax.ShapeDtypeStruct((classes, rows), kind),
        in_specs=[stored] * 8,
        out_specs=pl.BlockSpec(memory_space=pltpu.VMEM),
        scratch_shapes=scratch,
        compiler_params=pltpu.CompilerParams(
            collective_id=0, has_side_effects=True, vmem_limit_bytes=held
        ),
    )(
        *[
            pltpu.with_memory_space_constraint(value, pltpu.HBM)
            for value in (
                posterior.T, affinity.T, band_tiles, far_tiles, offset, count, far_row, far_block
            )
        ]
    )
    return result.T


def solution(mesh):
    spread = ("gx", "gy")
    in_specs = (
        P(spread, None), P(spread, None), P(spread, None, None, None), P(spread, None),
        P(spread), P(spread, None, None, None), P(spread, None), P(spread, None),
    )

    def run(posterior, affinity, band_tiles, offset, count, far_tiles, far_row, far_block):
        return local(
            mesh.shape["gx"], mesh.shape["gy"],
            posterior, affinity, band_tiles, offset, count, far_tiles, far_row, far_block,
        )

    return jax.shard_map(run, mesh=mesh, in_specs=in_specs, out_specs=P(spread, None), check_vma=False)
```

```python
import functools

import jax
import jax.numpy as jnp
from jax import lax
from jax.experimental import pallas as pl
from jax.experimental.pallas import tpu as pltpu
from jax.sharding import PartitionSpec as P

SWEEPS = 2
propagation_weight = 0.9
epsilon = 1e-06
SHARE = 0.352
HALVES = 1
DIRECT = 1
BRIDGE = 1
MESH = pl.DeviceIdType.MESH


def partner(me, step, peers):
    total = 0
    bit = 1
    while bit < peers:
        here = lax.rem(me // bit, 2)
        total = total + bit * (lax.rem(here + 1, 2) if step & bit else here)
        bit *= 2
    return total


def split(first, size, pieces):
    step = -(-size // (pieces * 16)) * 16
    return [(c, min(step, first + size - c)) for c in range(first, first + size, step)]


def chunks_of(classes, peers):
    cuts = []
    first = 0
    if peers == 4:
        share = int(classes * SHARE) // 16 * 16
        if share:
            for via in (1, 2):
                cuts += [(c, w, via) for c, w in split(first, share, HALVES)]
                first += share
    cuts += [(c, w, 0) for c, w in split(first, classes - first, DIRECT)]
    return cuts


def kernel(
    peers, ring, cuts,
    post, aff_hbm, band_hbm, far_hbm, boff_hbm, bcnt_hbm, frow_hbm, fblk_hbm,
    out,
    own, exts, raws, pairs, stage, arrived, gauge, scale_gauge, asked, aff, band, far, near_weights, far_weights, acc,
    boff, bcnt, frow, fblk, own_scale, far_scale_out, far_scale_in,
    local_sem, ask_sem, pair_sem, halo_recv, far_recv, scale_sem, ready,
):
    me = lax.axis_index("gx")
    spot = lax.axis_index("gy")
    up = lax.rem(spot + 1, ring)
    down = lax.rem(spot + ring - 1, ring)
    blocks, slots, tile, _ = band.shape
    classes = post.shape[0]
    steps = sorted(range(1, peers), key=lambda r: (-bin(r).count("1"), r))
    mates = {r: partner(me, r, peers) for r in range(peers)}
    order = list(range(len(cuts)))
    early = [k for k, cut in enumerate(cuts) if cut[2]]

    barrier = pltpu.get_barrier_semaphore()
    for r in steps:
        pl.semaphore_signal(barrier, inc=1, device_id={"gx": mates[r]}, device_id_type=MESH)

    def greet(sem, side, when):
        @pl.when(when)
        def _():
            pl.semaphore_signal(sem, inc=1, device_id={"gy": side}, device_id_type=MESH)

    greet(barrier, up, spot < ring - 1)
    greet(barrier, down, spot == 0)

    pending = []
    pair_send, halo_send, far_send, scale_send = (
        local_sem.at[0], [local_sem.at[1], local_sem.at[2]],
        [local_sem.at[3], local_sem.at[6], local_sem.at[4]], local_sem.at[5],
    )

    def load(source, target):
        copy = pltpu.make_async_copy(source, target, local_sem.at[len(pending)])
        copy.start()
        pending.append(copy)
        return copy

    for b in range(blocks):
        pltpu.make_async_copy(post.at[:, pl.ds(b * tile, tile)], own[0].at[b], local_sem.at[0]).start()
    pending.append(None)
    words = [
        load(source, target)
        for source, target in ((fblk_hbm, fblk), (frow_hbm, frow), (bcnt_hbm, bcnt), (boff_hbm, boff))
    ]
    band_load = load(band_hbm, band)
    far_load = load(far_hbm, far)
    aff_load = load(aff_hbm, aff)

    def drain(whole, sem):
        pltpu.make_async_copy(whole, whole, sem).wait()

    def several(copies, first, size):
        return gauge.at[pl.ds(0, copies), pl.ds(first, size)]

    def to_mate(r, source, target, send, recv):
        return pltpu.make_async_remote_copy(
            src_ref=source, dst_ref=target, send_sem=send, recv_sem=recv,
            device_id={"gx": mates[r]}, device_id_type=MESH,
        )

    def to_sides(first, last, before, after, send, recv):
        for source, target, side in ((last, before, up), (first, after, down)):
            pltpu.make_async_remote_copy(
                src_ref=source, dst_ref=target, send_sem=send, recv_sem=recv,
                device_id={"gy": side}, device_id_type=MESH,
            ).start()

    def flock(sweep, k):
        return sweep + 1 if sweep else min(k, 1)

    def send_halo(sweep, k):
        c, w, _ = cuts[k]
        to_sides(
            own[sweep].at[0, pl.ds(c, w)], own[sweep].at[blocks - 1, pl.ds(c, w)],
            exts[sweep][k].at[0], exts[sweep][k].at[blocks + 1],
            halo_send[sweep], halo_recv.at[flock(sweep, k)],
        )

    def send_far(sweep, k, mates_of):
        c, w, _ = cuts[k]
        rows = pl.ds(c, w)
        for r in mates_of:
            if sweep and k < BRIDGE:
                stage[sweep, r, rows, :] = raws[k][wanted[r]]
            else:
                stage[sweep, r, rows, :] = own[sweep][wanted[r], rows, :]
            to_mate(
                r, stage.at[sweep, r, rows], arrived.at[sweep, r, rows],
                far_send[SWEEPS if sweep == 0 and cuts[k][2] else sweep], far_recv.at[sweep, k],
            ).start()

    pl.semaphore_wait(
        barrier, len(steps) + jnp.where(spot == 0, 0, 1) + jnp.where(spot == ring - 1, 1, 0)
    )

    def ask(r):
        to_mate(r, fblk_hbm, asked.at[r], ask_sem.at[0], ask_sem.at[r]).start()

    near_mates = [r for r in steps if r & (r - 1) == 0]
    other_mates = [r for r in steps if r not in near_mates]
    for r in near_mates:
        ask(r)
    drain(own[0], local_sem.at[0])
    for k in early:
        c, w, via = cuts[k]
        to_mate(
            via, own[0].at[:, pl.ds(c, w)], pairs[k], pair_send, pair_sem.at[early.index(k)]
        ).start()
    for r in other_mates:
        ask(r)
    greet(ready.at[0], down, spot > 0)
    greet(ready.at[1], up, spot == ring - 1)
    for k, (c, w, _) in enumerate(cuts):
        for b in range(blocks):
            exts[0][k][1 + b] = own[0][b, pl.ds(c, w), :]
    for copy in words:
        copy.wait()
    for i, when in enumerate((spot < ring - 1, spot == 0)):
        @pl.when(when)
        def _():
            pl.semaphore_wait(ready.at[i], 1)
    for k in order:
        send_halo(0, k)

    wanted = {}

    def hear(mates_of):
        for r in mates_of:
            to_mate(r, fblk_hbm, asked.at[r], ask_sem.at[0], ask_sem.at[r]).wait_recv()
            wanted[r] = asked[r, 0, me]

    hear(near_mates)
    for k in early:
        send_far(0, k, [3 - cuts[k][2]])

    def weights(scaled):
        if not scaled:
            for b in range(blocks):
                for s in range(slots):
                    part = band[b, s].astype(jnp.float32) * jnp.where(s < bcnt[b], 1.0, 0.0)
                    near_weights[b, pl.ds(s * tile, tile), :] = part.astype(jnp.bfloat16).T
        for r in range(peers):
            part = far[0, mates[r]]
            if scaled and r:
                part = (part.astype(jnp.float32) * far_scale_in[r][0:1, :]).astype(jnp.bfloat16)
            part = part.T
            home = frow[0, mates[r]]
            for b in range(blocks):
                chosen = jnp.where(home == b, 1.0, 0.0).astype(jnp.bfloat16)
                far_weights[scaled, pl.ds(r * tile, tile), pl.ds(b * tile, tile)] = part * chosen

    band_load.wait()
    far_load.wait()
    weights(0)
    hear(other_mates)
    for k in order:
        if k not in early:
            send_far(0, k, other_mates)
    aff_load.wait()

    for i, k in enumerate(early):
        c, w, via = cuts[k]
        rows = pl.ds(c, w)
        over = 3 - via
        drain(pairs[k], pair_sem.at[i])
        stage[0, 3, rows, :] = pairs[k][asked[over, 0, mates[via]]]
        to_mate(
            over, stage.at[0, 3, rows], arrived.at[0, 3, rows], far_send[SWEEPS], far_recv.at[0, k]
        ).start()
    for k in order:
        if k not in early:
            send_far(0, k, [r for r in steps if r in near_mates])

    def keep(sweep, k):
        c, w, _ = cuts[k]
        for b in range(blocks):
            value = acc[pl.ds(c, w), pl.ds(b * tile, tile)] * scale[:, b * tile : (b + 1) * tile]
            value = value.astype(jnp.bfloat16)
            own[sweep][b, pl.ds(c, w), :] = value
            exts[sweep][k][1 + b] = value

    for sweep in range(SWEEPS):
        squares = jnp.zeros((1, blocks * tile), jnp.float32)
        for k in order:
            c, w, via = cuts[k]
            rows = pl.ds(c, w)
            if sweep == 0 and k == 0:
                drain(several(2, c, w), halo_recv.at[0])
            if sweep == 0 and k == 1:
                drain(several(2, c, classes - c), halo_recv.at[1])
            if sweep > 0 and k == 0:
                drain(several(2, 0, classes), halo_recv.at[2])
            near = [
                jnp.dot(
                    jnp.concatenate(
                        [exts[sweep][k][b + 1 + boff[b, s]] for s in range(slots)], axis=1
                    ),
                    near_weights[b], preferred_element_type=jnp.float32,
                )
                for b in range(blocks)
            ]
            early_here = sweep == 0 and via
            raw = sweep > 0 and k < BRIDGE
            if raw and k == 0:
                drain(scale_gauge, scale_sem.at[0])
                weights(1)
            drain(several(peers - 1 - (1 if early_here else 0), c, w), far_recv.at[sweep, k])
            parts = [own[sweep][fblk[0, me], rows, :]]
            for r in range(1, peers):
                if early_here and r == via:
                    parts.append(pairs[k][fblk[0, mates[r]]])
                else:
                    parts.append(arrived[sweep, r, rows, :])
            mixed = jnp.dot(
                jnp.concatenate(parts, axis=1), far_weights[1 if raw else 0],
                preferred_element_type=jnp.float32,
            )
            mixed = mixed + jnp.concatenate(near, axis=1)
            mixed = propagation_weight * mixed + aff[rows, :].astype(jnp.float32)
            squares += jnp.sum(mixed * mixed, axis=0, keepdims=True)
            acc[rows, :] = mixed
            if sweep < SWEEPS - 1 and k < BRIDGE:
                for b in range(blocks):
                    raws[k][b] = mixed[:, b * tile : (b + 1) * tile].astype(jnp.bfloat16)
                send_far(sweep + 1, k, steps)
        scale = lax.rsqrt(squares / classes + epsilon)
        if sweep == SWEEPS - 1:
            for c, w, _ in cuts:
                out[pl.ds(c, w), :] = (acc[pl.ds(c, w), :] * scale).astype(jnp.bfloat16)
            continue
        for b in range(blocks):
            own_scale[b] = jnp.broadcast_to(scale[:, b * tile : (b + 1) * tile], (8, tile))
        for r in steps:
            far_scale_out[r] = own_scale[wanted[r]]
        for r in steps:
            to_mate(
                r, far_scale_out.at[r], far_scale_in.at[r], scale_send, scale_sem.at[0]
            ).start()
        for k in order:
            keep(sweep + 1, k)
            send_halo(sweep + 1, k)
            if k >= BRIDGE:
                send_far(sweep + 1, k, steps)

    for r in steps:
        to_mate(r, fblk_hbm, asked.at[r], ask_sem.at[0], ask_sem.at[r]).wait_send()
    relayed = sum(w for _, w, via in cuts if via)
    if early:
        drain(own[0].at[:, pl.ds(0, relayed)], pair_send)
        drain(several(2, 0, relayed), far_send[SWEEPS])
    drain(several(peers - 1, relayed, classes - relayed), far_send[0])
    drain(several(peers - 1, 0, classes), far_send[1])
    for sweep in range(SWEEPS):
        drain(several(2, 0, classes), halo_send[sweep])
    drain(scale_gauge, scale_send)


def local(peers, ring, posterior, affinity, band_tiles, offset, count, far_tiles, far_row, far_block):
    rows, classes = posterior.shape
    blocks, slots, tile, _ = band_tiles.shape
    stored = pl.BlockSpec(memory_space=pltpu.HBM)
    kind = jnp.bfloat16
    cuts = chunks_of(classes, peers)
    pieces = len(cuts)
    early = sum(1 for cut in cuts if cut[2])
    scratch = [
        [pltpu.VMEM((blocks, classes, tile), kind)] * SWEEPS,
        [[pltpu.VMEM((blocks + 2, w, tile), kind) for _, w, _ in cuts] for _ in range(SWEEPS)],
        [pltpu.VMEM((blocks, w, tile), kind) for _, w, _ in cuts[:BRIDGE]],
        [pltpu.VMEM((blocks, w if via else 16, tile), kind) for _, w, via in cuts],
        pltpu.VMEM((SWEEPS, peers, classes, tile), kind),
        pltpu.VMEM((SWEEPS, peers, classes, tile), kind),
        pltpu.VMEM((max(peers - 1, 2), classes, tile), kind),
        pltpu.VMEM((peers - 1, 8, tile), jnp.float32),
        pltpu.SMEM((peers,) + far_block.shape, jnp.int32),
        pltpu.VMEM((classes, rows), kind),
        pltpu.VMEM(band_tiles.shape, kind),
        pltpu.VMEM(far_tiles.shape, kind),
        pltpu.VMEM((blocks, slots * tile, tile), kind),
        pltpu.VMEM((2, peers * tile, rows), kind),
        pltpu.VMEM((classes, rows), jnp.float32),
        pltpu.SMEM(offset.shape, jnp.int32),
        pltpu.SMEM(count.shape, jnp.int32),
        pltpu.SMEM(far_row.shape, jnp.int32),
        pltpu.SMEM(far_block.shape, jnp.int32),
        pltpu.VMEM((blocks, 8, tile), jnp.float32),
        pltpu.VMEM((peers, 8, tile), jnp.float32),
        pltpu.VMEM((peers, 8, tile), jnp.float32),
        pltpu.SemaphoreType.DMA((8,)),
        pltpu.SemaphoreType.DMA((peers,)),
        pltpu.SemaphoreType.DMA((max(early, 1),)),
        pltpu.SemaphoreType.DMA((SWEEPS + 1,)),
        pltpu.SemaphoreType.DMA((SWEEPS, pieces)),
        pltpu.SemaphoreType.DMA((1,)),
        pltpu.SemaphoreType.REGULAR((2,)),
    ]
    held = min(8 * rows * classes * (3 + 2 * peers) + 24 * 2**20, 60 * 2**20)
    result = pl.pallas_call(
        functools.partial(kernel, peers, ring, cuts),
        out_shape=jax.ShapeDtypeStruct((classes, rows), kind),
        in_specs=[stored] * 8,
        out_specs=pl.BlockSpec(memory_space=pltpu.VMEM),
        scratch_shapes=scratch,
        compiler_params=pltpu.CompilerParams(
            collective_id=0, has_side_effects=True, vmem_limit_bytes=held
        ),
    )(
        *[
            pltpu.with_memory_space_constraint(value, pltpu.HBM)
            for value in (
                posterior.T, affinity.T, band_tiles, far_tiles, offset, count, far_row, far_block
            )
        ]
    )
    return result.T


def solution(mesh):
    spread = ("gx", "gy")
    in_specs = (
        P(spread, None), P(spread, None), P(spread, None, None, None), P(spread, None),
        P(spread), P(spread, None, None, None), P(spread, None), P(spread, None),
    )

    def run(posterior, affinity, band_tiles, offset, count, far_tiles, far_row, far_block):
        return local(
            mesh.shape["gx"], mesh.shape["gy"],
            posterior, affinity, band_tiles, offset, count, far_tiles, far_row, far_block,
        )

    return jax.shard_map(run, mesh=mesh, in_specs=in_specs, out_specs=P(spread, None), check_vma=False)
```
